32 devices in a mesh: cls: 16 (over z, y, x), dp: 2 (over core).
Axes of the slice: x: 2, y: 2, z: 4, core: 2. Of those that a mesh axis runs over, the one named last changes fastest.
Arguments:
- images: bfloat16 [512, 4096], P(('cls', 'dp')), may hold values from -6 to 6
- references: bfloat16 [16, 72, 4096], P('cls'), may hold values from -1 to 1
- candidates: int32 [512, 8], P(('cls', 'dp')), may hold values from 0 to 15, all different within a row; in each aligned block of 16 rows (0 to 15, 16 to 31, ...) at most 12 rows name the same one
- inv_noise: bfloat16 [512], P(('cls', 'dp')), may hold values from 0.5 to 150
Outputs:
- class_sums: float32 [16, 72, 4096], P('cls', 'dp')
- class_weights: float32 [16, 72], P('cls', 'dp')
The draws below stay inside these ranges and needn't reach their ends.
Inputs may be any that keep to these rules, and one draw needn't show every extreme that they name: `candidates`: the classes of one row differ. In each aligned block of 16 rows (the rows of one device) no class is named by more than 12 rows, a bound that some block reaches.
All inputs are finite; a program needn't handle non-finite values.
Results may differ from the reference program's by a relative error of at most 0.006.
Values may be sent and summed in bfloat16 or wider, within the bound.
A program may use at most 64 MiB of HBM per device.

```python
import math
import jax
import jax.numpy as jnp
import numpy as np
from jax import lax

PIX = 64
ROTS = 72
SHIFTS = 9
TOP = 8
P_DEV = 16
IMG = 4096
CLASSES = 16
PARTICLES = 512
MOST = 12
N_CLS = 16
N_DP = 2


def draw_references(key, part):
    key_base, key_scale = jax.random.split(jax.random.fold_in(key, 17))
    base_draw = jax.random.normal(key_base, (CLASSES, ROTS, IMG), jnp.float32)
    row_scale = jnp.exp(jax.random.uniform(key_scale, (CLASSES, ROTS, 1), jnp.float32, jnp.log(0.5), jnp.log(2.0)))
    values = jnp.clip(base_draw * row_scale * IMG ** (-0.5), -1.0, 1.0)
    return values.astype(jnp.bfloat16)


def draw_inv_noise(key, part):
    key_base = jax.random.fold_in(jax.random.fold_in(key, 29), 0)
    values = jnp.exp(jax.random.uniform(key_base, (PARTICLES,), jnp.float32, jnp.log(0.5), jnp.log(3.0)))
    return values.astype(jnp.bfloat16)


def level_of(key, shape, shards, least, largest):
    factor_of, own = 1.0, jax.random.fold_in(key, 6)
    for dim, shards_of in shards:
        steps = jnp.exp(jax.random.uniform(jax.random.fold_in(own, dim), (shards_of,), jnp.float32, least / len(shards), largest / len(shards)))
        factor_of = factor_of * jnp.repeat(steps, shape[dim] // shards_of).reshape([-1 if axis == dim else 1 for axis in range(len(shape))])
    return factor_of


def routed_block(key, own, number, rows, count, top, reach, skew):
    order = jax.random.permutation(key, count)
    crowded, usual = portions_of(count, rows * top, reach, skew, True), portions_of(count, rows * top, reach, skew, False)
    places = jnp.arange(count)

    def named(sizes, rotation):
        used = int((sizes > 0).sum())
        fixed = max(1, used // 4)
        passed = fixed + (places - fixed + rotation * (used - fixed)) % max(1, count - fixed)
        return jnp.zeros((count,), jnp.int32).at[order[jnp.where(places < fixed, places, passed)]].set(jnp.asarray(sizes, jnp.int32))

    sizes = jnp.where(number % 4 == 0, named(crowded, number // 4), named(usual, number - number // 4 - 1))
    mixed = jax.random.permutation(jax.random.fold_in(own, 3), count)
    donor, taker = mixed[0:count // 2 * 2:2], mixed[1:count // 2 * 2:2]
    margin = jnp.minimum(sizes[donor] - 1, reach - sizes[taker]) // 2
    margin = jnp.where((donor == order[0]) | (taker == order[0]) | (sizes[taker] == 0), 0, jnp.maximum(margin, 0))
    passed = jax.random.randint(jax.random.fold_in(own, 4), (count // 2,), 0, 1 << 20) % (margin + 1)
    sizes = sizes.at[donor].add(-passed).at[taker].add(passed)
    members = jnp.searchsorted(jnp.cumsum(sizes), jnp.arange(rows * top), side="right").astype(jnp.int32)
    table = members.reshape(top, rows).T
    table = table[jax.random.permutation(jax.random.fold_in(own, 1), rows)]
    rotation = jax.random.randint(jax.random.fold_in(own, 2), (rows, 1), 0, top)
    return jnp.take_along_axis(table, (jnp.arange(top)[None, :] + rotation) % top, axis=1)


def portions_of(count, total, most, slope, full):
    weights = [(1 << 20) // math.isqrt(rank ** slope) + 1 for rank in range(1, count + 1)]
    largest = most if full else min(most, max(-(-total // count), total * weights[0] // sum(weights)))
    least = 1 if total - largest >= count - 1 else 0
    holding, rest = [largest] + [least] * (count - 1), total - largest - least * (count - 1)
    while rest > 0:
        free = [i for i in range(1, count) if holding[i] < largest] or [i for i in range(1, count) if holding[i] < most]
        pool, remaining = sum([weights[i] for i in free]), rest
        for i in free:
            addition = min(most - holding[i], max(1, remaining * weights[i] // pool), rest)
            holding[i] = holding[i] + addition
            rest = rest - addition
    return np.array(holding)


def centred(stream_key, shape, spread, limit, cuts=(), held_as=jnp.bfloat16):
    drawn = jax.random.normal(stream_key, shape, jnp.float32) * spread
    if len(cuts) > 0:
        drawn = level_of(stream_key, shape, cuts, -0.22, 0.18) * drawn
    return jnp.clip(drawn, min=-limit, max=limit).astype(held_as)


def setup_inputs(seed: int = 0) -> dict:
    key_of = jax.random.split(jax.random.key(seed), 5)
    images = centred(key_of[0], (PARTICLES, IMG), 1.0, 6.0, ((0, 32),))
    references = draw_references(jax.random.fold_in(key_of[4], 71), 0)
    candidates_keys = jax.random.split(jax.random.fold_in(key_of[2], 1), PARTICLES // P_DEV)
    candidates_turns = jax.random.permutation(jax.random.fold_in(key_of[2], 3), PARTICLES // P_DEV)
    candidates = jax.vmap(lambda own, number: routed_block(jax.random.fold_in(key_of[2], 2), own, number, P_DEV, CLASSES, TOP, MOST, 2))(candidates_keys, candidates_turns).reshape((PARTICLES, TOP))
    inv_noise = draw_inv_noise(jax.random.fold_in(key_of[4], 71), 0)
    return {"images": images, "references": references, "candidates": candidates, "inv_noise": inv_noise}


OFFSETS = ((0, 0), (1, 0), (-1, 0), (0, 1), (0, -1), (1, 1), (1, -1), (-1, 1), (-1, -1))


def shift_stack(rotated):
    square = rotated.reshape(ROTS, PIX, PIX)
    stacked = jnp.stack([jnp.roll(square, (shift_row, shift_col), axis=(1, 2)) for shift_row, shift_col in OFFSETS], axis=1)
    return stacked.reshape(ROTS * SHIFTS, IMG)


def unshift_sum(summed_back):
    square = summed_back.reshape(ROTS, SHIFTS, PIX, PIX)
    result = jnp.zeros((ROTS, PIX, PIX), jnp.float32)
    for position, offset in enumerate(OFFSETS):
        result = result + jnp.roll(square[:, position], (-offset[0], -offset[1]), axis=(1, 2))
    return result.reshape(ROTS, IMG)


def reference(images, references, candidates, inv_noise):
    capacity = MOST * N_CLS * N_DP
    rows_all = jnp.arange(PARTICLES, dtype=jnp.int32)
    member = jnp.zeros((PARTICLES, CLASSES), jnp.int32).at[rows_all[:, None], candidates].add(1)
    before = jnp.cumsum(member, axis=0) - member
    slot_rank = jnp.take_along_axis(before, candidates, axis=1)
    precision = inv_noise.astype(jnp.float32)

    def entries(class_id):
        in_class = member[:, class_id] > 0
        entry_rows = jnp.nonzero(in_class, size=capacity, fill_value=0)[0].astype(jnp.int32)
        is_live = jnp.arange(capacity, dtype=jnp.int32) < jnp.sum(in_class.astype(jnp.int32))
        return entry_rows, is_live

    def score_class(class_id):
        entry_rows, is_live = entries(class_id)
        entry_images = images[entry_rows]
        rotated = lax.dynamic_index_in_dim(references, class_id, 0, keepdims=False)
        shifted = shift_stack(rotated)
        ref_norms = jnp.sum(jnp.square(rotated.astype(jnp.float32)), axis=1)
        products = lax.dot_general(entry_images, shifted, (((1,), (1,)), ((), ())), preferred_element_type=jnp.float32)
        return precision[entry_rows][:, None] * (products - 0.5 * jnp.repeat(ref_norms, SHIFTS)[None, :])

    scores = lax.map(score_class, jnp.arange(CLASSES, dtype=jnp.int32))
    slot_peak = jnp.max(scores, axis=-1)
    slot_sum = jnp.sum(jnp.exp(scores - slot_peak[..., None]), axis=-1)
    home_peaks = slot_peak[candidates, slot_rank]
    home_sums = slot_sum[candidates, slot_rank]
    row_peak = jnp.max(home_peaks, axis=1)
    norm_total = jnp.sum(home_sums * jnp.exp(home_peaks - row_peak[:, None]), axis=1)

    def back_class(class_id):
        entry_rows, is_live = entries(class_id)
        entry_images = images[entry_rows]
        class_scores = lax.dynamic_index_in_dim(scores, class_id, 0, keepdims=False)
        entry_weights = (jnp.exp(class_scores - row_peak[entry_rows][:, None]) / norm_total[entry_rows][:, None]).astype(jnp.bfloat16)
        entry_weights = jnp.where(is_live[:, None], entry_weights, jnp.zeros_like(entry_weights))
        summed_back = lax.dot_general(entry_weights, entry_images, (((0,), (0,)), ((), ())), preferred_element_type=jnp.float32)
        weight_tot = jnp.sum(entry_weights.astype(jnp.float32), axis=0).reshape(ROTS, SHIFTS).sum(axis=1)
        return unshift_sum(summed_back), weight_tot

    class_sums, class_weights = lax.map(back_class, jnp.arange(CLASSES, dtype=jnp.int32))
    return class_sums, class_weights
```

```python
import functools
import math

import jax
import jax.numpy as jnp
from jax import lax
from jax.experimental import pallas as pl
from jax.experimental.pallas import tpu as pltpu
from jax.sharding import PartitionSpec as P

MESH = pl.DeviceIdType.MESH
LANES = 128
LOW = -1e30

OFFSETS = ((0, 0), (1, 0), (-1, 0), (0, 1), (0, -1), (1, 1), (1, -1), (-1, 1), (-1, -1))


def roll_flat(rows, shift_row, shift_col, side_len):
    result = jnp.roll(rows, shift_row * side_len, axis=1)
    if shift_col != 0:
        column = jnp.arange(side_len * side_len, dtype=jnp.int32) % side_len
        edge = 0 if shift_col > 0 else side_len - 1
        wrapped = jnp.roll(result, shift_col - shift_col * side_len, axis=1)
        plain = jnp.roll(result, shift_col, axis=1)
        result = jnp.where((column == edge)[None, :], wrapped, plain)
    return result


def shift_stack(rotated, side_len):
    return jnp.concatenate(
        [roll_flat(rotated, shift_row, shift_col, side_len) for shift_row, shift_col in OFFSETS],
        axis=0,
    )


def unshift_sum(summed_back, rot_count, side_len):
    square = summed_back.reshape(len(OFFSETS), rot_count, side_len * side_len)
    result = jnp.zeros((rot_count, side_len * side_len), jnp.float32)
    for position, offset in enumerate(OFFSETS):
        result = result + roll_flat(square[position], -offset[0], -offset[1], side_len)
    return result


def on_device(images, references, candidates, inv_noise):
    rows_dev, top_count = candidates.shape
    cls_dev, rot_count, pixels = references.shape
    side_len = math.isqrt(pixels)
    shift_count = len(OFFSETS)
    orient_count = rot_count * shift_count
    n_cls = lax.axis_size("cls")
    classes = cls_dev * n_cls
    slot_depth = max(2, (3 * rows_dev * top_count + 2 * classes - 1) // (2 * classes))
    owner_slots = cls_dev * slot_depth
    slots_all = n_cls * owner_slots
    member = jnp.sum(
        (candidates[:, :, None] == jnp.arange(classes, dtype=jnp.int32)[None, None, :]).astype(
            jnp.int32
        ),
        axis=1,
    )
    before = jnp.cumsum(member, axis=0) - member
    slot_rank = jnp.take_along_axis(before, candidates, axis=1)
    slot_index = candidates // cls_dev * owner_slots + candidates % cls_dev * slot_depth + slot_rank
    flat_slot = slot_index.reshape(-1)
    source = (
        jnp.full((slots_all,), rows_dev, jnp.int32)
        .at[flat_slot]
        .set(jnp.repeat(jnp.arange(rows_dev, dtype=jnp.int32), top_count))
    )
    images_pad = jnp.concatenate([images, jnp.zeros((1, pixels), jnp.bfloat16)], axis=0)
    noise_pad = jnp.concatenate([inv_noise, jnp.zeros((1,), jnp.bfloat16)], axis=0)
    send_img = images_pad[source].reshape(n_cls, owner_slots * pixels)
    send_noise = noise_pad[source].reshape(n_cls, owner_slots)
    recv_img, recv_noise = (
        lax.all_to_all(send_img, "cls", split_axis=0, concat_axis=0, tiled=True),
        lax.all_to_all(send_noise, "cls", split_axis=0, concat_axis=0, tiled=True),
    )
    live_list = []
    class_pos = 0
    rows_img = recv_img.reshape(n_cls * slot_depth, pixels)
    rows_noise = recv_noise.reshape(-1).astype(jnp.float32)
    shifted = shift_stack(references[class_pos], side_len)
    ref_norms = jnp.sum(jnp.square(references[class_pos].astype(jnp.float32)), axis=1)
    products = lax.dot_general(
        rows_img, shifted, (((1,), (1,)), ((), ())), preferred_element_type=jnp.float32
    )
    class_scores = rows_noise[:, None] * (
        products - 0.5 * jnp.tile(ref_norms, shift_count)[None, :]
    )
    rows_list = [rows_img]
    live_list.append(rows_noise > 0)
    score_list = [class_scores]
    send_scores = jnp.concatenate(
        [part_scores.reshape(n_cls, slot_depth * orient_count) for part_scores in score_list],
        axis=1,
    )
    home_scores = lax.all_to_all(send_scores, "cls", split_axis=0, concat_axis=0, tiled=True)
    own_scores = home_scores.reshape(slots_all, orient_count)[slot_index]
    row_peak = jnp.max(own_scores, axis=(1, 2))
    norm_total = jnp.sum(jnp.exp(own_scores - row_peak[:, None, None]), axis=(1, 2))
    home_weights = (
        jnp.exp(own_scores - row_peak[:, None, None]) / norm_total[:, None, None]
    ).astype(jnp.bfloat16)
    slot_weights = (
        jnp.zeros((slots_all, orient_count), jnp.bfloat16)
        .at[flat_slot]
        .set(home_weights.reshape(-1, orient_count))
    )
    weights = lax.all_to_all(
        slot_weights.reshape(n_cls, owner_slots * orient_count),
        "cls",
        split_axis=0,
        concat_axis=0,
        tiled=True,
    )
    weight_rows = [weights.reshape(n_cls * slot_depth, orient_count)]
    class_pos = 0
    row_weights = weight_rows[class_pos]
    summed_back = lax.dot_general(
        row_weights,
        rows_list[class_pos],
        (((0,), (0,)), ((), ())),
        preferred_element_type=jnp.float32,
    )
    sums_list = [unshift_sum(summed_back, rot_count, side_len)]
    weight_list = [
        jnp.sum(row_weights.astype(jnp.float32), axis=0).reshape(shift_count, rot_count).sum(axis=0)
    ]
    local_sums = jnp.stack(sums_list, axis=0)
    local_weights = jnp.stack(weight_list, axis=0)
    class_sums, class_weights = (
        lax.psum_scatter(local_sums, "dp", scatter_dimension=1, tiled=True),
        lax.psum_scatter(local_weights, "dp", scatter_dimension=1, tiled=True),
    )
    return (class_sums, class_weights)


PLANES = 4


def dense_kernel(
    rows_dev, pixels, half, pad, side, n_cls,
    own_ref, ref_ref, sums_ref, tot_ref,
    held, shifted, norms, acc, expo, back, mine, stats,
    own_sem, col_send, col_recv, x_send, y_send, a_recv, b_recv, part_send, part_recv,
    st_send, st_recv,
):
    cls = lax.axis_index("cls")
    d = lax.axis_index("dp")
    z, y, x = cls // 4, (cls // 2) % 2, cls % 2
    other = 1 - d
    me = cls * 2 + d
    n_dev = n_cls * 2
    width = held.shape[2]
    cut = (width // 2 + LANES - 1) // LANES * LANES
    part_a, part_b = pl.ds(0, cut), pl.ds(cut, width - cut)

    def block(bz, by, bx):
        return bz * 4 + by * 2 + bx

    barrier = pltpu.get_barrier_semaphore()

    def greet(j, carry):
        t = (me + j) % n_dev
        pl.semaphore_signal(barrier, inc=1, device_id={"cls": t // 2, "dp": t % 2}, device_id_type=MESH)
        return carry

    lax.fori_loop(1, n_dev, greet, 0)
    pl.semaphore_wait(barrier, n_dev - 1)

    t = z // 2
    order = [z, z + 1 - 2 * (z % 2), 2 - t, 3 - 3 * t]
    x_dev = {"cls": block(z, y, 1 - x), "dp": d}
    y_dev = {"cls": block(z, 1 - y, x), "dp": d}
    up_dev = {"cls": jnp.minimum(cls + 4, n_cls - 1) * 0 + (cls + 4) % n_cls, "dp": d}
    down_dev = {"cls": (cls + n_cls - 4) % n_cls, "dp": d}
    core_dev = {"cls": cls, "dp": other}

    def slot(b):
        return d * n_cls + b

    def remote(src, dst, send, recv, dev):
        return pltpu.make_async_remote_copy(
            src_ref=src, dst_ref=dst, send_sem=send, recv_sem=recv, device_id=dev, device_id_type=MESH
        )

    def full(k, which, b, dev):
        src = own_ref if k == 0 else held.at[slot(b)]
        return remote(src, held.at[slot(b)], col_send.at[k, which], col_recv.at[b], dev)

    def to_core(index, b, src=None):
        src = held.at[slot(b)] if src is None else src
        return remote(src, held.at[slot(b)], part_send.at[index], part_recv.at[b], core_dev)

    def piece(b, cols, send, recv, dev):
        ref = held.at[slot(b), :, cols]
        return remote(ref, ref, send, recv.at[b], dev)

    started = []

    def go(copy, cond=None):
        started.append((copy, cond))
        if cond is None:
            copy.start()
        else:
            pl.when(cond)(lambda: copy.start())

    def column_sends(k):
        b = block(order[k], y, x)
        zk = order[k]
        if k == 0:
            up, down = z < PLANES - 1, z > 0
        else:
            up = jnp.logical_and(zk < z, z < PLANES - 1)
            down = jnp.logical_and(zk > z, z > 0)
        go(full(k, 2, b, up_dev), up)
        go(full(k, 3, b, down_dev), down)
        go(full(k, 0, b, x_dev))
        go(full(k, 1, b, y_dev))
        go(to_core(k, b, own_ref if k == 0 else None))

    count = len(OFFSETS)

    def pick_rows():
        row = lax.broadcasted_iota(jnp.int32, (pad, 2 * half), 0)
        col = lax.broadcasted_iota(jnp.int32, (pad, 2 * half), 1)
        pick = jnp.logical_and(col == row + d * half, row < half).astype(jnp.float32).astype(jnp.bfloat16)
        width_c = pixels // 8
        for c in range(8):
            cols = pl.ds(c * width_c, width_c)
            back[0:pad, cols] = jnp.dot(pick, ref_ref[0, :, cols], preferred_element_type=jnp.float32)
        norms[...] = jnp.broadcast_to(
            jnp.sum(jnp.square(back[0:pad, :]), axis=1, keepdims=True), norms.shape
        )

    lane = lax.broadcasted_iota(jnp.int32, (8, pixels), 1) % side

    def rolled(v, dy, dx):
        amount = (dy * side) % pixels
        if dx == 0:
            return v if amount == 0 else pltpu.roll(v, amount, 1)
        plain = pltpu.roll(v, (dy * side + dx) % pixels, 1)
        wrapped = pltpu.roll(v, (dy * side + dx - dx * side) % pixels, 1)
        return jnp.where(lane == (0 if dx > 0 else side - 1), wrapped, plain)

    def build(positions):
        for pair in positions:
            group = [p for p in (2 * pair, 2 * pair + 1) if p < count]
            tiles = []
            for p in group:
                for i in range(pad // 8):
                    tiles.append((p, i))
            if len(tiles) % 2:
                tiles.append(None)
            for q in range(0, len(tiles), 2):
                parts = []
                for item in tiles[q:q + 2]:
                    if item is None:
                        parts.append(jnp.zeros((8, pixels), jnp.float32))
                    else:
                        p, i = item
                        parts.append(rolled(back[8 * i:8 * i + 8, :], *OFFSETS[p]))
                base = 2 * pair * pad + 8 * q
                shifted[base:base + 16, :] = jnp.concatenate(parts, axis=0).astype(jnp.bfloat16)

    local = pltpu.make_async_copy(own_ref, held.at[slot(cls)], own_sem)
    local.start()
    column_sends(0)
    pick_rows()
    build([0])
    for k in range(PLANES):
        xb = block(order[k], y, 1 - x)
        full(k, 0, xb, x_dev).wait_recv() if k else remote(held.at[slot(xb)], held.at[slot(xb)], col_send.at[0, 0], col_recv.at[xb], x_dev).wait_recv()
        go(piece(xb, part_b, x_send.at[k], b_recv, y_dev))
        go(to_core(PLANES + k, xb))
        yb = block(order[k], 1 - y, x)
        remote(held.at[slot(yb)], held.at[slot(yb)], col_send.at[0, 1], col_recv.at[yb], y_dev).wait_recv()
        go(piece(yb, part_a, y_send.at[k], a_recv, x_dev))
        go(to_core(2 * PLANES + k, yb))
        if k + 1 < PLANES:
            zb = block(order[k + 1], y, x)
            remote(held.at[slot(zb)], held.at[slot(zb)], col_send.at[0, 2], col_recv.at[zb], up_dev).wait_recv()
            column_sends(k + 1)
        build([k + 1])
    for k in range(PLANES):
        b = block(order[k], 1 - y, 1 - x)
        piece(b, part_a, y_send.at[k], a_recv, x_dev).wait_recv()
        piece(b, part_b, x_send.at[k], b_recv, y_dev).wait_recv()
        go(to_core(3 * PLANES + k, b))
    local.wait()

    def core_arrival(b, carry):
        s = other * n_cls + b
        remote(held.at[s], held.at[s], part_send.at[0], part_recv.at[b], core_dev).wait_recv()
        return carry

    lax.fori_loop(0, n_cls, core_arrival, 0)
    for copy, cond in started:
        if cond is None:
            copy.wait_send()
        else:
            pl.when(cond)(lambda copy=copy: copy.wait_send())

    n_all = n_dev * rows_dev
    height = shifted.shape[0]
    meta = held[:, :, pixels:pixels + LANES].reshape(n_all, LANES)
    pick = (lax.broadcasted_iota(jnp.int32, (8, LANES), 1) == cls).astype(jnp.float32).astype(jnp.bfloat16)
    noise = lax.dot_general(pick, meta, (((1,), (1,)), ((), ())), preferred_element_type=jnp.float32)[0:1, :]
    depth = pixels // 8

    acc[...] = jnp.zeros_like(acc)

    def chunk(c, carry):
        cols = pl.ds(pl.multiple_of(c * depth, depth), depth)
        right = held[:, :, cols].reshape(n_all, depth)
        acc[...] += lax.dot_general(
            shifted[:, cols], right, (((1,), (1,)), ((), ())), preferred_element_type=jnp.float32
        )
        return carry

    lax.fori_loop(0, 8, chunk, 0)
    rows = count * pad
    prod = acc[0:rows, :].reshape(count, pad, n_all)
    offset = 0.5 * norms[:, 0:1]
    valid = jnp.logical_and(
        noise[None] > 0,
        lax.broadcasted_iota(jnp.int32, (1, pad, n_all), 1) < half,
    )
    score = jnp.where(valid, noise[None] * (prod - offset[None]), LOW)
    peak = jnp.max(jnp.max(score, axis=0), axis=0, keepdims=True)
    grown = jnp.where(valid, jnp.exp(score - peak[None]), 0.0)
    total = jnp.sum(jnp.sum(grown, axis=0), axis=0, keepdims=True)
    mine[0:1, :] = peak
    mine[1:2, :] = total
    expo[...] = grown

    def stat(j):
        t = (me + j) % n_dev
        return remote(mine, stats.at[me], st_send.at[j], st_recv.at[me], {"cls": t // 2, "dp": t % 2})

    def send_stat(j, carry):
        stat(j).start()
        return carry

    stats[me] = mine[...]
    lax.fori_loop(1, n_dev, send_stat, 0)

    def wait_stat(j, carry):
        t = (me + j) % n_dev
        remote(mine, stats.at[t], st_send.at[j], st_recv.at[t], {"cls": t // 2, "dp": t % 2}).wait_recv()
        return carry

    lax.fori_loop(1, n_dev, wait_stat, 0)

    every = stats[...]
    peaks, totals = every[:, 0:1, :], every[:, 1:2, :]
    top = jnp.max(peaks, axis=0)
    norm = jnp.sum(totals * jnp.exp(peaks - top[None]), axis=0)
    factor = jnp.exp(mine[0:1, :] - top) / norm
    weight = (expo[...] * factor[None]).reshape(rows, n_all)
    if height > rows:
        weight = jnp.concatenate([weight, jnp.zeros((height - rows, n_all), jnp.float32)], axis=0)
    weight = weight.astype(jnp.bfloat16)
    flat = jnp.sum(weight[0:rows].astype(jnp.float32).reshape(count, pad, n_all), axis=0)
    column = jnp.sum(flat, axis=1, keepdims=True)
    eye = lax.broadcasted_iota(jnp.int32, (pad, LANES), 0) == lax.broadcasted_iota(jnp.int32, (pad, LANES), 1)
    tot_ref[...] = jnp.sum(jnp.where(eye, column, 0.0), axis=0, keepdims=True)[:, 0:half]
    shifted[:, 0:n_all] = weight

    def project(c, carry):
        cols = pl.ds(pl.multiple_of(c * depth, depth), depth)
        right = held[:, :, cols].reshape(n_all, depth)
        back[:, cols] = jnp.dot(shifted[:, 0:n_all], right, preferred_element_type=jnp.float32)
        return carry

    lax.fori_loop(0, 8, project, 0)

    place = {offset: i for i, offset in enumerate(OFFSETS)}

    def tile(i):
        lines = []
        for dx in (0, 1, -1):
            line = None
            for dy in (0, 1, -1):
                base = place[(dy, dx)] * pad + 8 * i
                term = rolled(back[base:base + 8, :], -dy, 0)
                line = term if line is None else line + term
            lines.append(line)
        return lines[0] + rolled(lines[1], 0, -1) + rolled(lines[2], 0, 1)

    for i in range(pad // 8):
        keep = min(8, half - 8 * i)
        sums_ref[0, 8 * i:8 * i + keep, :] = tile(i)[0:keep]

    def end_stat(j, carry):
        stat(j).wait_send()
        return carry

    lax.fori_loop(1, n_dev, end_stat, 0)


def dense_on_device(images, references, candidates, inv_noise):
    rows_dev, pixels = images.shape
    n_cls, n_dp = lax.axis_size("cls"), lax.axis_size("dp")
    rot_count = references.shape[1]
    half = rot_count // n_dp
    pad = (half + 7) // 8 * 8
    side = math.isqrt(pixels)
    height = (len(OFFSETS) * pad + 15) // 16 * 16
    n_all = rows_dev * n_cls * n_dp
    named = (candidates[:, :, None] == jnp.arange(LANES, dtype=jnp.int32)[None, None, :]).any(axis=1)
    meta = jnp.where(named, inv_noise[:, None], jnp.zeros((), jnp.bfloat16))
    own = jnp.concatenate([images, meta], axis=1)
    width = pixels + LANES
    dma = pltpu.SemaphoreType.DMA
    vmem = pl.BlockSpec(memory_space=pltpu.VMEM)
    return pl.pallas_call(
        functools.partial(dense_kernel, rows_dev, pixels, half, pad, side, n_cls),
        out_shape=(
            jax.ShapeDtypeStruct((1, half, pixels), jnp.float32),
            jax.ShapeDtypeStruct((1, half), jnp.float32),
        ),
        in_specs=[vmem, vmem],
        out_specs=(vmem, vmem),
        scratch_shapes=[
            pltpu.VMEM((n_cls * n_dp, rows_dev, width), jnp.bfloat16),
            pltpu.VMEM((height, pixels), jnp.bfloat16),
            pltpu.VMEM((pad, LANES), jnp.float32),
            pltpu.VMEM((height, n_all), jnp.float32),
            pltpu.VMEM((len(OFFSETS), pad, n_all), jnp.float32),
            pltpu.VMEM((height, pixels), jnp.float32),
            pltpu.VMEM((2, n_all), jnp.float32),
            pltpu.VMEM((n_cls * n_dp, 2, n_all), jnp.float32),
            dma,
            dma((PLANES, 4)),
            dma((n_cls,)),
            dma((PLANES,)),
            dma((PLANES,)),
            dma((n_cls,)),
            dma((n_cls,)),
            dma((4 * PLANES,)),
            dma((n_cls,)),
            dma((n_cls * n_dp,)),
            dma((n_cls * n_dp,)),
        ],
        compiler_params=pltpu.CompilerParams(
            collective_id=0, has_side_effects=True, vmem_limit_bytes=56 << 20
        ),
    )(own, references)


def solution(mesh):
    placed = (
        P(("cls", "dp"), None),
        P("cls", None, None),
        P(("cls", "dp"), None),
        P(("cls", "dp")),
    )
    n_cls, n_dp = mesh.shape["cls"], mesh.shape["dp"]
    dense = n_cls == PLANES * 4 and n_dp == 2
    return jax.shard_map(
        dense_on_device if dense else on_device,
        mesh=mesh,
        in_specs=placed,
        out_specs=(P("cls", "dp", None), P("cls", "dp")),
        check_vma=False,
    )
```

```python
import functools
import math

import jax
import jax.numpy as jnp
from jax import lax
from jax.experimental import pallas as pl
from jax.experimental.pallas import tpu as pltpu
from jax.sharding import PartitionSpec as P

MESH = pl.DeviceIdType.MESH
LANES = 128
LOW = -1e30

OFFSETS = ((0, 0), (1, 0), (-1, 0), (0, 1), (0, -1), (1, 1), (1, -1), (-1, 1), (-1, -1))


def roll_flat(rows, shift_row, shift_col, side_len):
    result = jnp.roll(rows, shift_row * side_len, axis=1)
    if shift_col != 0:
        column = jnp.arange(side_len * side_len, dtype=jnp.int32) % side_len
        edge = 0 if shift_col > 0 else side_len - 1
        wrapped = jnp.roll(result, shift_col - shift_col * side_len, axis=1)
        plain = jnp.roll(result, shift_col, axis=1)
        result = jnp.where((column == edge)[None, :], wrapped, plain)
    return result


def shift_stack(rotated, side_len):
    return jnp.concatenate(
        [roll_flat(rotated, shift_row, shift_col, side_len) for shift_row, shift_col in OFFSETS],
        axis=0,
    )


def unshift_sum(summed_back, rot_count, side_len):
    square = summed_back.reshape(len(OFFSETS), rot_count, side_len * side_len)
    result = jnp.zeros((rot_count, side_len * side_len), jnp.float32)
    for position, offset in enumerate(OFFSETS):
        result = result + roll_flat(square[position], -offset[0], -offset[1], side_len)
    return result


def on_device(images, references, candidates, inv_noise):
    rows_dev, top_count = candidates.shape
    cls_dev, rot_count, pixels = references.shape
    side_len = math.isqrt(pixels)
    shift_count = len(OFFSETS)
    orient_count = rot_count * shift_count
    n_cls = lax.axis_size("cls")
    classes = cls_dev * n_cls
    slot_depth = max(2, (3 * rows_dev * top_count + 2 * classes - 1) // (2 * classes))
    owner_slots = cls_dev * slot_depth
    slots_all = n_cls * owner_slots
    member = jnp.sum(
        (candidates[:, :, None] == jnp.arange(classes, dtype=jnp.int32)[None, None, :]).astype(
            jnp.int32
        ),
        axis=1,
    )
    before = jnp.cumsum(member, axis=0) - member
    slot_rank = jnp.take_along_axis(before, candidates, axis=1)
    slot_index = candidates // cls_dev * owner_slots + candidates % cls_dev * slot_depth + slot_rank
    flat_slot = slot_index.reshape(-1)
    source = (
        jnp.full((slots_all,), rows_dev, jnp.int32)
        .at[flat_slot]
        .set(jnp.repeat(jnp.arange(rows_dev, dtype=jnp.int32), top_count))
    )
    images_pad = jnp.concatenate([images, jnp.zeros((1, pixels), jnp.bfloat16)], axis=0)
    noise_pad = jnp.concatenate([inv_noise, jnp.zeros((1,), jnp.bfloat16)], axis=0)
    send_img = images_pad[source].reshape(n_cls, owner_slots * pixels)
    send_noise = noise_pad[source].reshape(n_cls, owner_slots)
    recv_img, recv_noise = (
        lax.all_to_all(send_img, "cls", split_axis=0, concat_axis=0, tiled=True),
        lax.all_to_all(send_noise, "cls", split_axis=0, concat_axis=0, tiled=True),
    )
    live_list = []
    class_pos = 0
    rows_img = recv_img.reshape(n_cls * slot_depth, pixels)
    rows_noise = recv_noise.reshape(-1).astype(jnp.float32)
    shifted = shift_stack(references[class_pos], side_len)
    ref_norms = jnp.sum(jnp.square(references[class_pos].astype(jnp.float32)), axis=1)
    products = lax.dot_general(
        rows_img, shifted, (((1,), (1,)), ((), ())), preferred_element_type=jnp.float32
    )
    class_scores = rows_noise[:, None] * (
        products - 0.5 * jnp.tile(ref_norms, shift_count)[None, :]
    )
    rows_list = [rows_img]
    live_list.append(rows_noise > 0)
    score_list = [class_scores]
    send_scores = jnp.concatenate(
        [part_scores.reshape(n_cls, slot_depth * orient_count) for part_scores in score_list],
        axis=1,
    )
    home_scores = lax.all_to_all(send_scores, "cls", split_axis=0, concat_axis=0, tiled=True)
    own_scores = home_scores.reshape(slots_all, orient_count)[slot_index]
    row_peak = jnp.max(own_scores, axis=(1, 2))
    norm_total = jnp.sum(jnp.exp(own_scores - row_peak[:, None, None]), axis=(1, 2))
    home_weights = (
        jnp.exp(own_scores - row_peak[:, None, None]) / norm_total[:, None, None]
    ).astype(jnp.bfloat16)
    slot_weights = (
        jnp.zeros((slots_all, orient_count), jnp.bfloat16)
        .at[flat_slot]
        .set(home_weights.reshape(-1, orient_count))
    )
    weights = lax.all_to_all(
        slot_weights.reshape(n_cls, owner_slots * orient_count),
        "cls",
        split_axis=0,
        concat_axis=0,
        tiled=True,
    )
    weight_rows = [weights.reshape(n_cls * slot_depth, orient_count)]
    class_pos = 0
    row_weights = weight_rows[class_pos]
    summed_back = lax.dot_general(
        row_weights,
        rows_list[class_pos],
        (((0,), (0,)), ((), ())),
        preferred_element_type=jnp.float32,
    )
    sums_list = [unshift_sum(summed_back, rot_count, side_len)]
    weight_list = [
        jnp.sum(row_weights.astype(jnp.float32), axis=0).reshape(shift_count, rot_count).sum(axis=0)
    ]
    local_sums = jnp.stack(sums_list, axis=0)
    local_weights = jnp.stack(weight_list, axis=0)
    class_sums, class_weights = (
        lax.psum_scatter(local_sums, "dp", scatter_dimension=1, tiled=True),
        lax.psum_scatter(local_weights, "dp", scatter_dimension=1, tiled=True),
    )
    return (class_sums, class_weights)


PLANES = 4


def dense_kernel(
    rows_dev, pixels, half, pad, side, n_cls,
    own_ref, ref_ref, sums_ref, tot_ref,
    held, shifted, norms, acc, expo, back, mine, stats,
    own_sem, col_send, col_recv, x_send, y_send, a_recv, b_recv, part_send, part_recv,
    st_send, st_recv,
):
    cls = lax.axis_index("cls")
    d = lax.axis_index("dp")
    z, y, x = cls // 4, (cls // 2) % 2, cls % 2
    other = 1 - d
    me = cls * 2 + d
    n_dev = n_cls * 2
    width = held.shape[2]
    cut = (width // 2 + LANES - 1) // LANES * LANES
    part_a, part_b = pl.ds(0, cut), pl.ds(cut, width - cut)

    def block(bz, by, bx):
        return bz * 4 + by * 2 + bx

    barrier = pltpu.get_barrier_semaphore()


    t = z // 2
    order = [z, z + 1 - 2 * (z % 2), 2 - t, 3 - 3 * t]
    x_dev = {"cls": block(z, y, 1 - x), "dp": d}
    y_dev = {"cls": block(z, 1 - y, x), "dp": d}
    up_dev = {"cls": (cls + 4) % n_cls, "dp": d}
    down_dev = {"cls": (cls + n_cls - 4) % n_cls, "dp": d}
    core_dev = {"cls": cls, "dp": other}

    def greet(dev):
        pl.semaphore_signal(barrier, inc=1, device_id=dev, device_id_type=MESH)

    for dev in (x_dev, y_dev, core_dev):
        greet(dev)
    pl.when(z < PLANES - 1)(lambda: greet(up_dev))
    pl.when(z > 0)(lambda: greet(down_dev))
    lines = 5 - jnp.where(z == 0, 1, 0) - jnp.where(z == PLANES - 1, 1, 0)
    pl.semaphore_wait(barrier, lines)

    def slot(b):
        return d * n_cls + b

    def remote(src, dst, send, recv, dev):
        return pltpu.make_async_remote_copy(
            src_ref=src, dst_ref=dst, send_sem=send, recv_sem=recv, device_id=dev, device_id_type=MESH
        )

    def full(k, which, b, dev):
        src = own_ref if k == 0 else held.at[slot(b)]
        return remote(src, held.at[slot(b)], col_send.at[k, which], col_recv.at[b], dev)

    def to_core(index, b, src=None):
        src = held.at[slot(b)] if src is None else src
        return remote(src, held.at[slot(b)], part_send.at[index], part_recv.at[b], core_dev)

    def piece(b, cols, send, recv, dev):
        ref = held.at[slot(b), :, cols]
        return remote(ref, ref, send, recv.at[b], dev)

    started = []

    def go(copy, cond=None):
        started.append((copy, cond))
        if cond is None:
            copy.start()
        else:
            pl.when(cond)(lambda: copy.start())

    def column_sends(k):
        b = block(order[k], y, x)
        zk = order[k]
        if k == 0:
            up, down = z < PLANES - 1, z > 0
        else:
            up = jnp.logical_and(zk < z, z < PLANES - 1)
            down = jnp.logical_and(zk > z, z > 0)
        go(full(k, 2, b, up_dev), up)
        go(full(k, 3, b, down_dev), down)
        go(full(k, 0, b, x_dev))
        go(full(k, 1, b, y_dev))
        go(to_core(k, b, own_ref if k == 0 else None))

    count = len(OFFSETS)

    def pick_rows():
        row = lax.broadcasted_iota(jnp.int32, (pad, 2 * half), 0)
        col = lax.broadcasted_iota(jnp.int32, (pad, 2 * half), 1)
        pick = jnp.logical_and(col == row + d * half, row < half).astype(jnp.float32).astype(jnp.bfloat16)
        width_c = pixels // 8
        for c in range(8):
            cols = pl.ds(c * width_c, width_c)
            back[0:pad, cols] = jnp.dot(pick, ref_ref[0, :, cols], preferred_element_type=jnp.float32)
        norms[...] = jnp.broadcast_to(
            jnp.sum(jnp.square(back[0:pad, :]), axis=1, keepdims=True), norms.shape
        )

    lane = lax.broadcasted_iota(jnp.int32, (8, pixels), 1) % side

    def rolled(v, dy, dx):
        amount = (dy * side) % pixels
        if dx == 0:
            return v if amount == 0 else pltpu.roll(v, amount, 1)
        plain = pltpu.roll(v, (dy * side + dx) % pixels, 1)
        wrapped = pltpu.roll(v, (dy * side + dx - dx * side) % pixels, 1)
        return jnp.where(lane == (0 if dx > 0 else side - 1), wrapped, plain)

    def build(positions):
        for pair in positions:
            group = [p for p in (2 * pair, 2 * pair + 1) if p < count]
            tiles = []
            for p in group:
                for i in range(pad // 8):
                    tiles.append((p, i))
            if len(tiles) % 2:
                tiles.append(None)
            for q in range(0, len(tiles), 2):
                parts = []
                for item in tiles[q:q + 2]:
                    if item is None:
                        parts.append(jnp.zeros((8, pixels), jnp.float32))
                    else:
                        p, i = item
                        parts.append(rolled(back[8 * i:8 * i + 8, :], *OFFSETS[p]))
                base = 2 * pair * pad + 8 * q
                shifted[base:base + 16, :] = jnp.concatenate(parts, axis=0).astype(jnp.bfloat16)

    local = pltpu.make_async_copy(own_ref, held.at[slot(cls)], own_sem)
    local.start()
    column_sends(0)
    pick_rows()
    build([0])
    for k in range(PLANES):
        xb = block(order[k], y, 1 - x)
        full(k, 0, xb, x_dev).wait_recv() if k else remote(held.at[slot(xb)], held.at[slot(xb)], col_send.at[0, 0], col_recv.at[xb], x_dev).wait_recv()
        go(piece(xb, part_b, x_send.at[k], b_recv, y_dev))
        go(to_core(PLANES + k, xb))
        yb = block(order[k], 1 - y, x)
        remote(held.at[slot(yb)], held.at[slot(yb)], col_send.at[0, 1], col_recv.at[yb], y_dev).wait_recv()
        go(piece(yb, part_a, y_send.at[k], a_recv, x_dev))
        go(to_core(2 * PLANES + k, yb))
        if k + 1 < PLANES:
            zb = block(order[k + 1], y, x)
            remote(held.at[slot(zb)], held.at[slot(zb)], col_send.at[0, 2], col_recv.at[zb], up_dev).wait_recv()
            column_sends(k + 1)
        build([k + 1])
    for k in range(PLANES):
        b = block(order[k], 1 - y, 1 - x)
        piece(b, part_a, y_send.at[k], a_recv, x_dev).wait_recv()
        piece(b, part_b, x_send.at[k], b_recv, y_dev).wait_recv()
        go(to_core(3 * PLANES + k, b))
    local.wait()

    def core_arrival(b, carry):
        s = other * n_cls + b
        remote(held.at[s], held.at[s], part_send.at[0], part_recv.at[b], core_dev).wait_recv()
        return carry

    lax.fori_loop(0, n_cls, core_arrival, 0)
    for copy, cond in started:
        if cond is None:
            copy.wait_send()
        else:
            pl.when(cond)(lambda copy=copy: copy.wait_send())

    n_all = n_dev * rows_dev
    height = shifted.shape[0]
    meta = held[:, :, pixels:pixels + LANES].reshape(n_all, LANES)
    pick = (lax.broadcasted_iota(jnp.int32, (8, LANES), 1) == cls).astype(jnp.float32).astype(jnp.bfloat16)
    noise = lax.dot_general(pick, meta, (((1,), (1,)), ((), ())), preferred_element_type=jnp.float32)[0:1, :]
    depth = pixels // 8

    acc[...] = jnp.zeros_like(acc)

    def chunk(c, carry):
        cols = pl.ds(pl.multiple_of(c * depth, depth), depth)
        right = held[:, :, cols].reshape(n_all, depth)
        acc[...] += lax.dot_general(
            shifted[:, cols], right, (((1,), (1,)), ((), ())), preferred_element_type=jnp.float32
        )
        return carry

    lax.fori_loop(0, 8, chunk, 0)
    rows = count * pad
    prod = acc[0:rows, :].reshape(count, pad, n_all)
    offset = 0.5 * norms[:, 0:1]
    valid = jnp.logical_and(
        noise[None] > 0,
        lax.broadcasted_iota(jnp.int32, (1, pad, n_all), 1) < half,
    )
    score = jnp.where(valid, noise[None] * (prod - offset[None]), LOW)
    peak = jnp.max(jnp.max(score, axis=0), axis=0, keepdims=True)
    grown = jnp.where(valid, jnp.exp(score - peak[None]), 0.0)
    total = jnp.sum(jnp.sum(grown, axis=0), axis=0, keepdims=True)
    mine[0:1, :] = peak
    mine[1:2, :] = total
    expo[...] = grown

    def stat(j):
        t = (me + j) % n_dev
        return remote(mine, stats.at[me], st_send.at[j], st_recv.at[me], {"cls": t // 2, "dp": t % 2})

    def send_stat(j, carry):
        stat(j).start()
        return carry

    stats[me] = mine[...]
    lax.fori_loop(1, n_dev, send_stat, 0)

    def wait_stat(j, carry):
        t = (me + j) % n_dev
        remote(mine, stats.at[t], st_send.at[j], st_recv.at[t], {"cls": t // 2, "dp": t % 2}).wait_recv()
        return carry

    lax.fori_loop(1, n_dev, wait_stat, 0)

    every = stats[...]
    peaks, totals = every[:, 0:1, :], every[:, 1:2, :]
    top = jnp.max(peaks, axis=0)
    norm = jnp.sum(totals * jnp.exp(peaks - top[None]), axis=0)
    factor = jnp.exp(mine[0:1, :] - top) / norm
    weight = (expo[...] * factor[None]).reshape(rows, n_all)
    if height > rows:
        weight = jnp.concatenate([weight, jnp.zeros((height - rows, n_all), jnp.float32)], axis=0)
    weight = weight.astype(jnp.bfloat16)
    flat = jnp.sum(weight[0:rows].astype(jnp.float32).reshape(count, pad, n_all), axis=0)
    column = jnp.sum(flat, axis=1, keepdims=True)
    eye = lax.broadcasted_iota(jnp.int32, (pad, LANES), 0) == lax.broadcasted_iota(jnp.int32, (pad, LANES), 1)
    tot_ref[...] = jnp.sum(jnp.where(eye, column, 0.0), axis=0, keepdims=True)[:, 0:half]
    shifted[:, 0:n_all] = weight

    def project(c, carry):
        cols = pl.ds(pl.multiple_of(c * depth, depth), depth)
        right = held[:, :, cols].reshape(n_all, depth)
        back[:, cols] = jnp.dot(shifted[:, 0:n_all], right, preferred_element_type=jnp.float32)
        return carry

    lax.fori_loop(0, 8, project, 0)

    place = {offset: i for i, offset in enumerate(OFFSETS)}

    def tile(i):
        lines = []
        for dx in (0, 1, -1):
            line = None
            for dy in (0, 1, -1):
                base = place[(dy, dx)] * pad + 8 * i
                term = rolled(back[base:base + 8, :], -dy, 0)
                line = term if line is None else line + term
            lines.append(line)
        return lines[0] + rolled(lines[1], 0, -1) + rolled(lines[2], 0, 1)

    for i in range(pad // 8):
        keep = min(8, half - 8 * i)
        sums_ref[0, 8 * i:8 * i + keep, :] = tile(i)[0:keep]

    def end_stat(j, carry):
        stat(j).wait_send()
        return carry

    lax.fori_loop(1, n_dev, end_stat, 0)


def dense_on_device(images, references, candidates, inv_noise):
    rows_dev, pixels = images.shape
    n_cls, n_dp = lax.axis_size("cls"), lax.axis_size("dp")
    rot_count = references.shape[1]
    half = rot_count // n_dp
    pad = (half + 7) // 8 * 8
    side = math.isqrt(pixels)
    height = (len(OFFSETS) * pad + 15) // 16 * 16
    n_all = rows_dev * n_cls * n_dp
    named = (candidates[:, :, None] == jnp.arange(LANES, dtype=jnp.int32)[None, None, :]).any(axis=1)
    meta = jnp.where(named, inv_noise[:, None], jnp.zeros((), jnp.bfloat16))
    own = jnp.concatenate([images, meta], axis=1)
    width = pixels + LANES
    dma = pltpu.SemaphoreType.DMA
    vmem = pl.BlockSpec(memory_space=pltpu.VMEM)
    sums, totals = pl.pallas_call(
        functools.partial(dense_kernel, rows_dev, pixels, half, pad, side, n_cls),
        out_shape=(
            jax.ShapeDtypeStruct((1, half, pixels), jnp.float32),
            jax.ShapeDtypeStruct((1, half), jnp.float32),
        ),
        in_specs=[vmem, vmem],
        out_specs=(vmem, vmem),
        scratch_shapes=[
            pltpu.VMEM((n_cls * n_dp, rows_dev, width), jnp.bfloat16),
            pltpu.VMEM((height, pixels), jnp.bfloat16),
            pltpu.VMEM((pad, LANES), jnp.float32),
            pltpu.VMEM((height, n_all), jnp.float32),
            pltpu.VMEM((len(OFFSETS), pad, n_all), jnp.float32),
            pltpu.VMEM((height, pixels), jnp.float32),
            pltpu.VMEM((2, n_all), jnp.float32),
            pltpu.VMEM((n_cls * n_dp, 2, n_all), jnp.float32),
            dma,
            dma((PLANES, 4)),
            dma((n_cls,)),
            dma((PLANES,)),
            dma((PLANES,)),
            dma((n_cls,)),
            dma((n_cls,)),
            dma((4 * PLANES,)),
            dma((n_cls,)),
            dma((n_cls * n_dp,)),
            dma((n_cls * n_dp,)),
        ],
        compiler_params=pltpu.CompilerParams(
            collective_id=0, has_side_effects=True, vmem_limit_bytes=56 << 20
        ),
    )(own, references)
    return sums, totals


def solution(mesh):
    placed = (
        P(("cls", "dp"), None),
        P("cls", None, None),
        P(("cls", "dp"), None),
        P(("cls", "dp")),
    )
    n_cls, n_dp = mesh.shape["cls"], mesh.shape["dp"]
    dense = n_cls == PLANES * 4 and n_dp == 2
    return jax.shard_map(
        dense_on_device if dense else on_device,
        mesh=mesh,
        in_specs=placed,
        out_specs=(P("cls", "dp", None), P("cls", "dp")),
        check_vma=False,
    )
```

```python
import functools
import math

import jax
import jax.numpy as jnp
from jax import lax
from jax.experimental import pallas as pl
from jax.experimental.pallas import tpu as pltpu
from jax.sharding import PartitionSpec as P

MESH = pl.DeviceIdType.MESH
LANES = 128
LOW = -1e30

OFFSETS = ((0, 0), (1, 0), (-1, 0), (0, 1), (0, -1), (1, 1), (1, -1), (-1, 1), (-1, -1))


def roll_flat(rows, shift_row, shift_col, side_len):
    result = jnp.roll(rows, shift_row * side_len, axis=1)
    if shift_col != 0:
        column = jnp.arange(side_len * side_len, dtype=jnp.int32) % side_len
        edge = 0 if shift_col > 0 else side_len - 1
        wrapped = jnp.roll(result, shift_col - shift_col * side_len, axis=1)
        plain = jnp.roll(result, shift_col, axis=1)
        result = jnp.where((column == edge)[None, :], wrapped, plain)
    return result


def shift_stack(rotated, side_len):
    return jnp.concatenate(
        [roll_flat(rotated, shift_row, shift_col, side_len) for shift_row, shift_col in OFFSETS],
        axis=0,
    )


def unshift_sum(summed_back, rot_count, side_len):
    square = summed_back.reshape(len(OFFSETS), rot_count, side_len * side_len)
    result = jnp.zeros((rot_count, side_len * side_len), jnp.float32)
    for position, offset in enumerate(OFFSETS):
        result = result + roll_flat(square[position], -offset[0], -offset[1], side_len)
    return result


def on_device(images, references, candidates, inv_noise):
    rows_dev, top_count = candidates.shape
    cls_dev, rot_count, pixels = references.shape
    side_len = math.isqrt(pixels)
    shift_count = len(OFFSETS)
    orient_count = rot_count * shift_count
    n_cls = lax.axis_size("cls")
    classes = cls_dev * n_cls
    slot_depth = max(2, (3 * rows_dev * top_count + 2 * classes - 1) // (2 * classes))
    owner_slots = cls_dev * slot_depth
    slots_all = n_cls * owner_slots
    member = jnp.sum(
        (candidates[:, :, None] == jnp.arange(classes, dtype=jnp.int32)[None, None, :]).astype(
            jnp.int32
        ),
        axis=1,
    )
    before = jnp.cumsum(member, axis=0) - member
    slot_rank = jnp.take_along_axis(before, candidates, axis=1)
    slot_index = candidates // cls_dev * owner_slots + candidates % cls_dev * slot_depth + slot_rank
    flat_slot = slot_index.reshape(-1)
    source = (
        jnp.full((slots_all,), rows_dev, jnp.int32)
        .at[flat_slot]
        .set(jnp.repeat(jnp.arange(rows_dev, dtype=jnp.int32), top_count))
    )
    images_pad = jnp.concatenate([images, jnp.zeros((1, pixels), jnp.bfloat16)], axis=0)
    noise_pad = jnp.concatenate([inv_noise, jnp.zeros((1,), jnp.bfloat16)], axis=0)
    send_img = images_pad[source].reshape(n_cls, owner_slots * pixels)
    send_noise = noise_pad[source].reshape(n_cls, owner_slots)
    recv_img, recv_noise = (
        lax.all_to_all(send_img, "cls", split_axis=0, concat_axis=0, tiled=True),
        lax.all_to_all(send_noise, "cls", split_axis=0, concat_axis=0, tiled=True),
    )
    live_list = []
    class_pos = 0
    rows_img = recv_img.reshape(n_cls * slot_depth, pixels)
    rows_noise = recv_noise.reshape(-1).astype(jnp.float32)
    shifted = shift_stack(references[class_pos], side_len)
    ref_norms = jnp.sum(jnp.square(references[class_pos].astype(jnp.float32)), axis=1)
    products = lax.dot_general(
        rows_img, shifted, (((1,), (1,)), ((), ())), preferred_element_type=jnp.float32
    )
    class_scores = rows_noise[:, None] * (
        products - 0.5 * jnp.tile(ref_norms, shift_count)[None, :]
    )
    rows_list = [rows_img]
    live_list.append(rows_noise > 0)
    score_list = [class_scores]
    send_scores = jnp.concatenate(
        [part_scores.reshape(n_cls, slot_depth * orient_count) for part_scores in score_list],
        axis=1,
    )
    home_scores = lax.all_to_all(send_scores, "cls", split_axis=0, concat_axis=0, tiled=True)
    own_scores = home_scores.reshape(slots_all, orient_count)[slot_index]
    row_peak = jnp.max(own_scores, axis=(1, 2))
    norm_total = jnp.sum(jnp.exp(own_scores - row_peak[:, None, None]), axis=(1, 2))
    home_weights = (
        jnp.exp(own_scores - row_peak[:, None, None]) / norm_total[:, None, None]
    ).astype(jnp.bfloat16)
    slot_weights = (
        jnp.zeros((slots_all, orient_count), jnp.bfloat16)
        .at[flat_slot]
        .set(home_weights.reshape(-1, orient_count))
    )
    weights = lax.all_to_all(
        slot_weights.reshape(n_cls, owner_slots * orient_count),
        "cls",
        split_axis=0,
        concat_axis=0,
        tiled=True,
    )
    weight_rows = [weights.reshape(n_cls * slot_depth, orient_count)]
    class_pos = 0
    row_weights = weight_rows[class_pos]
    summed_back = lax.dot_general(
        row_weights,
        rows_list[class_pos],
        (((0,), (0,)), ((), ())),
        preferred_element_type=jnp.float32,
    )
    sums_list = [unshift_sum(summed_back, rot_count, side_len)]
    weight_list = [
        jnp.sum(row_weights.astype(jnp.float32), axis=0).reshape(shift_count, rot_count).sum(axis=0)
    ]
    local_sums = jnp.stack(sums_list, axis=0)
    local_weights = jnp.stack(weight_list, axis=0)
    class_sums, class_weights = (
        lax.psum_scatter(local_sums, "dp", scatter_dimension=1, tiled=True),
        lax.psum_scatter(local_weights, "dp", scatter_dimension=1, tiled=True),
    )
    return (class_sums, class_weights)


PLANES = 4


def dense_kernel(
    rows_dev, pixels, half, pad, side, n_cls,
    own_ref, ref_ref, sums_ref, tot_ref,
    held, shifted, norms, acc, expo, back, mine, stats,
    own_sem, col_send, col_recv, x_send, y_send, a_recv, b_recv, part_send, part_recv,
    st_send, st_recv,
):
    cls = lax.axis_index("cls")
    d = lax.axis_index("dp")
    z, y, x = cls // 4, (cls // 2) % 2, cls % 2
    other = 1 - d
    me = cls * 2 + d
    n_dev = n_cls * 2
    width = held.shape[2]
    cut = (width // 2 + LANES - 1) // LANES * LANES
    part_a, part_b = pl.ds(0, cut), pl.ds(cut, width - cut)

    def block(bz, by, bx):
        return bz * 4 + by * 2 + bx

    barrier = pltpu.get_barrier_semaphore()


    t = z // 2
    order = [z, z + 1 - 2 * (z % 2), 2 - t, 3 - 3 * t]
    x_dev = {"cls": block(z, y, 1 - x), "dp": d}
    y_dev = {"cls": block(z, 1 - y, x), "dp": d}
    up_dev = {"cls": (cls + 4) % n_cls, "dp": d}
    down_dev = {"cls": (cls + n_cls - 4) % n_cls, "dp": d}
    core_dev = {"cls": cls, "dp": other}

    def greet(dev):
        pl.semaphore_signal(barrier, inc=1, device_id=dev, device_id_type=MESH)

    for dev in (x_dev, y_dev, core_dev):
        greet(dev)
    pl.when(z < PLANES - 1)(lambda: greet(up_dev))
    pl.when(z > 0)(lambda: greet(down_dev))
    lines = 5 - jnp.where(z == 0, 1, 0) - jnp.where(z == PLANES - 1, 1, 0)
    pl.semaphore_wait(barrier, lines)

    def slot(b):
        return d * n_cls + b

    def remote(src, dst, send, recv, dev):
        return pltpu.make_async_remote_copy(
            src_ref=src, dst_ref=dst, send_sem=send, recv_sem=recv, device_id=dev, device_id_type=MESH
        )

    pieces = (part_a, part_b)

    def full(k, h, which, b, dev):
        src = own_ref if k == 0 else held.at[slot(b)]
        return remote(
            src.at[:, pieces[h]], held.at[slot(b), :, pieces[h]], col_send.at[k, h, which], col_recv.at[h, b], dev
        )

    def arrived(h, b, dev):
        ref = held.at[slot(b), :, pieces[h]]
        remote(ref, ref, col_send.at[0, h, 0], col_recv.at[h, b], dev).wait_recv()

    def to_core(index, b, src=None):
        src = held.at[slot(b)] if src is None else src
        return remote(src, held.at[slot(b)], part_send.at[index], part_recv.at[b], core_dev)

    def piece(b, cols, send, recv, dev):
        ref = held.at[slot(b), :, cols]
        return remote(ref, ref, send, recv.at[b], dev)

    started = []

    def go(copy, cond=None):
        started.append((copy, cond))
        if cond is None:
            copy.start()
        else:
            pl.when(cond)(lambda: copy.start())

    def column_sends(k, h):
        b = block(order[k], y, x)
        zk = order[k]
        if k == 0:
            up, down = z < PLANES - 1, z > 0
        else:
            up = jnp.logical_and(zk < z, z < PLANES - 1)
            down = jnp.logical_and(zk > z, z > 0)
        go(full(k, h, 2, b, up_dev), up)
        go(full(k, h, 3, b, down_dev), down)
        go(full(k, h, 0, b, x_dev))
        go(full(k, h, 1, b, y_dev))
        if h == 1:
            go(to_core(k, b, own_ref if k == 0 else None))

    count = len(OFFSETS)

    def pick_rows():
        row = lax.broadcasted_iota(jnp.int32, (pad, 2 * half), 0)
        col = lax.broadcasted_iota(jnp.int32, (pad, 2 * half), 1)
        pick = jnp.logical_and(col == row + d * half, row < half).astype(jnp.float32).astype(jnp.bfloat16)
        width_c = pixels // 8
        for c in range(8):
            cols = pl.ds(c * width_c, width_c)
            back[0:pad, cols] = jnp.dot(pick, ref_ref[0, :, cols], preferred_element_type=jnp.float32)
        norms[...] = jnp.broadcast_to(
            jnp.sum(jnp.square(back[0:pad, :]), axis=1, keepdims=True), norms.shape
        )

    lane = lax.broadcasted_iota(jnp.int32, (8, pixels), 1) % side

    def rolled(v, dy, dx):
        amount = (dy * side) % pixels
        if dx == 0:
            return v if amount == 0 else pltpu.roll(v, amount, 1)
        plain = pltpu.roll(v, (dy * side + dx) % pixels, 1)
        wrapped = pltpu.roll(v, (dy * side + dx - dx * side) % pixels, 1)
        return jnp.where(lane == (0 if dx > 0 else side - 1), wrapped, plain)

    def build(positions):
        for pair in positions:
            group = [p for p in (2 * pair, 2 * pair + 1) if p < count]
            tiles = []
            for p in group:
                for i in range(pad // 8):
                    tiles.append((p, i))
            if len(tiles) % 2:
                tiles.append(None)
            for q in range(0, len(tiles), 2):
                parts = []
                for item in tiles[q:q + 2]:
                    if item is None:
                        parts.append(jnp.zeros((8, pixels), jnp.float32))
                    else:
                        p, i = item
                        parts.append(rolled(back[8 * i:8 * i + 8, :], *OFFSETS[p]))
                base = 2 * pair * pad + 8 * q
                shifted[base:base + 16, :] = jnp.concatenate(parts, axis=0).astype(jnp.bfloat16)

    local = pltpu.make_async_copy(own_ref, held.at[slot(cls)], own_sem)
    local.start()
    column_sends(0, 0)
    column_sends(0, 1)
    pick_rows()
    build([0])
    for k in range(PLANES):
        xb = block(order[k], y, 1 - x)
        yb = block(order[k], 1 - y, x)
        for h in range(2):
            if k + 1 < PLANES:
                arrived(h, block(order[k + 1], y, x), up_dev)
                column_sends(k + 1, h)
            arrived(h, xb, x_dev)
            if h == 1:
                go(piece(xb, part_b, x_send.at[k], b_recv, y_dev))
                go(to_core(PLANES + k, xb))
            arrived(h, yb, y_dev)
            if h == 0:
                go(piece(yb, part_a, y_send.at[k], a_recv, x_dev))
            else:
                go(to_core(2 * PLANES + k, yb))
        build([k + 1])
    for k in range(PLANES):
        b = block(order[k], 1 - y, 1 - x)
        piece(b, part_a, y_send.at[k], a_recv, x_dev).wait_recv()
        piece(b, part_b, x_send.at[k], b_recv, y_dev).wait_recv()
        go(to_core(3 * PLANES + k, b))
    local.wait()

    def core_arrival(b, carry):
        s = other * n_cls + b
        remote(held.at[s], held.at[s], part_send.at[0], part_recv.at[b], core_dev).wait_recv()
        return carry

    lax.fori_loop(0, n_cls, core_arrival, 0)
    for copy, cond in started:
        if cond is None:
            copy.wait_send()
        else:
            pl.when(cond)(lambda copy=copy: copy.wait_send())

    n_all = n_dev * rows_dev
    height = shifted.shape[0]
    meta = held[:, :, pixels:pixels + LANES].reshape(n_all, LANES)
    pick = (lax.broadcasted_iota(jnp.int32, (8, LANES), 1) == cls).astype(jnp.float32).astype(jnp.bfloat16)
    noise = lax.dot_general(pick, meta, (((1,), (1,)), ((), ())), preferred_element_type=jnp.float32)[0:1, :]
    depth = pixels // 8

    acc[...] = jnp.zeros_like(acc)

    def chunk(c, carry):
        cols = pl.ds(pl.multiple_of(c * depth, depth), depth)
        right = held[:, :, cols].reshape(n_all, depth)
        acc[...] += lax.dot_general(
            shifted[:, cols], right, (((1,), (1,)), ((), ())), preferred_element_type=jnp.float32
        )
        return carry

    lax.fori_loop(0, 8, chunk, 0)
    rows = count * pad
    prod = acc[0:rows, :].reshape(count, pad, n_all)
    offset = 0.5 * norms[:, 0:1]
    valid = jnp.logical_and(
        noise[None] > 0,
        lax.broadcasted_iota(jnp.int32, (1, pad, n_all), 1) < half,
    )
    score = jnp.where(valid, noise[None] * (prod - offset[None]), LOW)
    peak = jnp.max(jnp.max(score, axis=0), axis=0, keepdims=True)
    grown = jnp.where(valid, jnp.exp(score - peak[None]), 0.0)
    total = jnp.sum(jnp.sum(grown, axis=0), axis=0, keepdims=True)
    mine[0:1, :] = peak
    mine[1:2, :] = total
    expo[...] = grown

    def stat(j):
        t = (me + j) % n_dev
        return remote(mine, stats.at[me], st_send.at[j], st_recv.at[me], {"cls": t // 2, "dp": t % 2})

    def send_stat(j, carry):
        stat(j).start()
        return carry

    stats[me] = mine[...]
    lax.fori_loop(1, n_dev, send_stat, 0)

    def wait_stat(j, carry):
        t = (me + j) % n_dev
        remote(mine, stats.at[t], st_send.at[j], st_recv.at[t], {"cls": t // 2, "dp": t % 2}).wait_recv()
        return carry

    lax.fori_loop(1, n_dev, wait_stat, 0)

    every = stats[...]
    peaks, totals = every[:, 0:1, :], every[:, 1:2, :]
    top = jnp.max(peaks, axis=0)
    norm = jnp.sum(totals * jnp.exp(peaks - top[None]), axis=0)
    factor = jnp.exp(mine[0:1, :] - top) / norm
    weight = (expo[...] * factor[None]).reshape(rows, n_all)
    if height > rows:
        weight = jnp.concatenate([weight, jnp.zeros((height - rows, n_all), jnp.float32)], axis=0)
    weight = weight.astype(jnp.bfloat16)
    flat = jnp.sum(weight[0:rows].astype(jnp.float32).reshape(count, pad, n_all), axis=0)
    column = jnp.sum(flat, axis=1, keepdims=True)
    eye = lax.broadcasted_iota(jnp.int32, (pad, LANES), 0) == lax.broadcasted_iota(jnp.int32, (pad, LANES), 1)
    tot_ref[...] = jnp.sum(jnp.where(eye, column, 0.0), axis=0, keepdims=True)[:, 0:half]
    shifted[:, 0:n_all] = weight

    def project(c, carry):
        cols = pl.ds(pl.multiple_of(c * depth, depth), depth)
        right = held[:, :, cols].reshape(n_all, depth)
        back[:, cols] = jnp.dot(shifted[:, 0:n_all], right, preferred_element_type=jnp.float32)
        return carry

    lax.fori_loop(0, 8, project, 0)

    place = {offset: i for i, offset in enumerate(OFFSETS)}

    def tile(i):
        lines = []
        for dx in (0, 1, -1):
            line = None
            for dy in (0, 1, -1):
                base = place[(dy, dx)] * pad + 8 * i
                term = rolled(back[base:base + 8, :], -dy, 0)
                line = term if line is None else line + term
            lines.append(line)
        return lines[0] + rolled(lines[1], 0, -1) + rolled(lines[2], 0, 1)

    for i in range(pad // 8):
        keep = min(8, half - 8 * i)
        sums_ref[0, 8 * i:8 * i + keep, :] = tile(i)[0:keep]

    def end_stat(j, carry):
        stat(j).wait_send()
        return carry

    lax.fori_loop(1, n_dev, end_stat, 0)


def dense_on_device(images, references, candidates, inv_noise):
    rows_dev, pixels = images.shape
    n_cls, n_dp = lax.axis_size("cls"), lax.axis_size("dp")
    rot_count = references.shape[1]
    half = rot_count // n_dp
    pad = (half + 7) // 8 * 8
    side = math.isqrt(pixels)
    height = (len(OFFSETS) * pad + 15) // 16 * 16
    n_all = rows_dev * n_cls * n_dp
    named = (candidates[:, :, None] == jnp.arange(LANES, dtype=jnp.int32)[None, None, :]).any(axis=1)
    meta = jnp.where(named, inv_noise[:, None], jnp.zeros((), jnp.bfloat16))
    own = jnp.concatenate([images, meta], axis=1)
    width = pixels + LANES
    dma = pltpu.SemaphoreType.DMA
    vmem = pl.BlockSpec(memory_space=pltpu.VMEM)
    sums, totals = pl.pallas_call(
        functools.partial(dense_kernel, rows_dev, pixels, half, pad, side, n_cls),
        out_shape=(
            jax.ShapeDtypeStruct((1, half, pixels), jnp.float32),
            jax.ShapeDtypeStruct((1, half), jnp.float32),
        ),
        in_specs=[vmem, vmem],
        out_specs=(vmem, vmem),
        scratch_shapes=[
            pltpu.VMEM((n_cls * n_dp, rows_dev, width), jnp.bfloat16),
            pltpu.VMEM((height, pixels), jnp.bfloat16),
            pltpu.VMEM((pad, LANES), jnp.float32),
            pltpu.VMEM((height, n_all), jnp.float32),
            pltpu.VMEM((len(OFFSETS), pad, n_all), jnp.float32),
            pltpu.VMEM((height, pixels), jnp.float32),
            pltpu.VMEM((2, n_all), jnp.float32),
            pltpu.VMEM((n_cls * n_dp, 2, n_all), jnp.float32),
            dma,
            dma((PLANES, 2, 4)),
            dma((2, n_cls)),
            dma((PLANES,)),
            dma((PLANES,)),
            dma((n_cls,)),
            dma((n_cls,)),
            dma((4 * PLANES,)),
            dma((n_cls,)),
            dma((n_cls * n_dp,)),
            dma((n_cls * n_dp,)),
        ],
        compiler_params=pltpu.CompilerParams(
            collective_id=0, has_side_effects=True, vmem_limit_bytes=56 << 20
        ),
    )(own, references)
    return sums, totals


def solution(mesh):
    placed = (
        P(("cls", "dp"), None),
        P("cls", None, None),
        P(("cls", "dp"), None),
        P(("cls", "dp")),
    )
    n_cls, n_dp = mesh.shape["cls"], mesh.shape["dp"]
    dense = n_cls == PLANES * 4 and n_dp == 2
    return jax.shard_map(
        dense_on_device if dense else on_device,
        mesh=mesh,
        in_specs=placed,
        out_specs=(P("cls", "dp", None), P("cls", "dp")),
        check_vma=False,
    )
```

```python
import functools
import math

import jax
import jax.numpy as jnp
from jax import lax
from jax.experimental import pallas as pl
from jax.experimental.pallas import tpu as pltpu
from jax.sharding import PartitionSpec as P

MESH = pl.DeviceIdType.MESH
LANES = 128
LOW = -1e30

OFFSETS = ((0, 0), (1, 0), (-1, 0), (0, 1), (0, -1), (1, 1), (1, -1), (-1, 1), (-1, -1))


def roll_flat(rows, shift_row, shift_col, side_len):
    result = jnp.roll(rows, shift_row * side_len, axis=1)
    if shift_col != 0:
        column = jnp.arange(side_len * side_len, dtype=jnp.int32) % side_len
        edge = 0 if shift_col > 0 else side_len - 1
        wrapped = jnp.roll(result, shift_col - shift_col * side_len, axis=1)
        plain = jnp.roll(result, shift_col, axis=1)
        result = jnp.where((column == edge)[None, :], wrapped, plain)
    return result


def shift_stack(rotated, side_len):
    return jnp.concatenate(
        [roll_flat(rotated, shift_row, shift_col, side_len) for shift_row, shift_col in OFFSETS],
        axis=0,
    )


def unshift_sum(summed_back, rot_count, side_len):
    square = summed_back.reshape(len(OFFSETS), rot_count, side_len * side_len)
    result = jnp.zeros((rot_count, side_len * side_len), jnp.float32)
    for position, offset in enumerate(OFFSETS):
        result = result + roll_flat(square[position], -offset[0], -offset[1], side_len)
    return result


def on_device(images, references, candidates, inv_noise):
    rows_dev, top_count = candidates.shape
    cls_dev, rot_count, pixels = references.shape
    side_len = math.isqrt(pixels)
    shift_count = len(OFFSETS)
    orient_count = rot_count * shift_count
    n_cls = lax.axis_size("cls")
    classes = cls_dev * n_cls
    slot_depth = max(2, (3 * rows_dev * top_count + 2 * classes - 1) // (2 * classes))
    owner_slots = cls_dev * slot_depth
    slots_all = n_cls * owner_slots
    member = jnp.sum(
        (candidates[:, :, None] == jnp.arange(classes, dtype=jnp.int32)[None, None, :]).astype(
            jnp.int32
        ),
        axis=1,
    )
    before = jnp.cumsum(member, axis=0) - member
    slot_rank = jnp.take_along_axis(before, candidates, axis=1)
    slot_index = candidates // cls_dev * owner_slots + candidates % cls_dev * slot_depth + slot_rank
    flat_slot = slot_index.reshape(-1)
    source = (
        jnp.full((slots_all,), rows_dev, jnp.int32)
        .at[flat_slot]
        .set(jnp.repeat(jnp.arange(rows_dev, dtype=jnp.int32), top_count))
    )
    images_pad = jnp.concatenate([images, jnp.zeros((1, pixels), jnp.bfloat16)], axis=0)
    noise_pad = jnp.concatenate([inv_noise, jnp.zeros((1,), jnp.bfloat16)], axis=0)
    send_img = images_pad[source].reshape(n_cls, owner_slots * pixels)
    send_noise = noise_pad[source].reshape(n_cls, owner_slots)
    recv_img, recv_noise = (
        lax.all_to_all(send_img, "cls", split_axis=0, concat_axis=0, tiled=True),
        lax.all_to_all(send_noise, "cls", split_axis=0, concat_axis=0, tiled=True),
    )
    live_list = []
    class_pos = 0
    rows_img = recv_img.reshape(n_cls * slot_depth, pixels)
    rows_noise = recv_noise.reshape(-1).astype(jnp.float32)
    shifted = shift_stack(references[class_pos], side_len)
    ref_norms = jnp.sum(jnp.square(references[class_pos].astype(jnp.float32)), axis=1)
    products = lax.dot_general(
        rows_img, shifted, (((1,), (1,)), ((), ())), preferred_element_type=jnp.float32
    )
    class_scores = rows_noise[:, None] * (
        products - 0.5 * jnp.tile(ref_norms, shift_count)[None, :]
    )
    rows_list = [rows_img]
    live_list.append(rows_noise > 0)
    score_list = [class_scores]
    send_scores = jnp.concatenate(
        [part_scores.reshape(n_cls, slot_depth * orient_count) for part_scores in score_list],
        axis=1,
    )
    home_scores = lax.all_to_all(send_scores, "cls", split_axis=0, concat_axis=0, tiled=True)
    own_scores = home_scores.reshape(slots_all, orient_count)[slot_index]
    row_peak = jnp.max(own_scores, axis=(1, 2))
    norm_total = jnp.sum(jnp.exp(own_scores - row_peak[:, None, None]), axis=(1, 2))
    home_weights = (
        jnp.exp(own_scores - row_peak[:, None, None]) / norm_total[:, None, None]
    ).astype(jnp.bfloat16)
    slot_weights = (
        jnp.zeros((slots_all, orient_count), jnp.bfloat16)
        .at[flat_slot]
        .set(home_weights.reshape(-1, orient_count))
    )
    weights = lax.all_to_all(
        slot_weights.reshape(n_cls, owner_slots * orient_count),
        "cls",
        split_axis=0,
        concat_axis=0,
        tiled=True,
    )
    weight_rows = [weights.reshape(n_cls * slot_depth, orient_count)]
    class_pos = 0
    row_weights = weight_rows[class_pos]
    summed_back = lax.dot_general(
        row_weights,
        rows_list[class_pos],
        (((0,), (0,)), ((), ())),
        preferred_element_type=jnp.float32,
    )
    sums_list = [unshift_sum(summed_back, rot_count, side_len)]
    weight_list = [
        jnp.sum(row_weights.astype(jnp.float32), axis=0).reshape(shift_count, rot_count).sum(axis=0)
    ]
    local_sums = jnp.stack(sums_list, axis=0)
    local_weights = jnp.stack(weight_list, axis=0)
    class_sums, class_weights = (
        lax.psum_scatter(local_sums, "dp", scatter_dimension=1, tiled=True),
        lax.psum_scatter(local_weights, "dp", scatter_dimension=1, tiled=True),
    )
    return (class_sums, class_weights)


PLANES = 4


def dense_kernel(
    rows_dev, pixels, half, pad, side, n_cls,
    own_ref, ref_ref, sums_ref, tot_ref,
    held, shifted, norms, acc, expo, back, mine, stats,
    own_sem, col_send, col_recv, x_send, y_send, a_recv, b_recv, part_send, part_recv,
    st_send, st_recv,
):
    cls = lax.axis_index("cls")
    d = lax.axis_index("dp")
    z, y, x = cls // 4, (cls // 2) % 2, cls % 2
    other = 1 - d
    me = cls * 2 + d
    n_dev = n_cls * 2
    width = held.shape[2]
    cut = (width // 2 + LANES - 1) // LANES * LANES
    part_a, part_b = pl.ds(0, cut), pl.ds(cut, width - cut)

    def block(bz, by, bx):
        return bz * 4 + by * 2 + bx

    barrier = pltpu.get_barrier_semaphore()


    t = z // 2
    order = [z, z + 1 - 2 * (z % 2), 2 - t, 3 - 3 * t]
    x_dev = {"cls": block(z, y, 1 - x), "dp": d}
    y_dev = {"cls": block(z, 1 - y, x), "dp": d}
    up_dev = {"cls": (cls + 4) % n_cls, "dp": d}
    down_dev = {"cls": (cls + n_cls - 4) % n_cls, "dp": d}
    core_dev = {"cls": cls, "dp": other}

    def greet(dev):
        pl.semaphore_signal(barrier, inc=1, device_id=dev, device_id_type=MESH)

    for dev in (x_dev, y_dev, core_dev):
        greet(dev)
    pl.when(z < PLANES - 1)(lambda: greet(up_dev))
    pl.when(z > 0)(lambda: greet(down_dev))
    lines = 5 - jnp.where(z == 0, 1, 0) - jnp.where(z == PLANES - 1, 1, 0)
    pl.semaphore_wait(barrier, lines)

    def slot(b):
        return d * n_cls + b

    def remote(src, dst, send, recv, dev):
        return pltpu.make_async_remote_copy(
            src_ref=src, dst_ref=dst, send_sem=send, recv_sem=recv, device_id=dev, device_id_type=MESH
        )

    pieces = (part_a, part_b)

    def full(k, h, which, b, dev):
        src = own_ref if k == 0 else held.at[slot(b)]
        return remote(
            src.at[:, pieces[h]], held.at[slot(b), :, pieces[h]], col_send.at[k, h, which], col_recv.at[h, b], dev
        )

    def arrived(h, b, dev):
        ref = held.at[slot(b), :, pieces[h]]
        remote(ref, ref, col_send.at[0, h, 0], col_recv.at[h, b], dev).wait_recv()

    def to_core(index, b, src=None):
        src = held.at[slot(b)] if src is None else src
        return remote(src, held.at[slot(b)], part_send.at[index], part_recv.at[b], core_dev)

    def piece(b, cols, send, recv, dev):
        ref = held.at[slot(b), :, cols]
        return remote(ref, ref, send, recv.at[b], dev)

    started = []

    def go(copy, cond=None):
        started.append((copy, cond))
        if cond is None:
            copy.start()
        else:
            pl.when(cond)(lambda: copy.start())

    def column_sends(k, h):
        b = block(order[k], y, x)
        zk = order[k]
        if k == 0:
            up, down = z < PLANES - 1, z > 0
        else:
            up = jnp.logical_and(zk < z, z < PLANES - 1)
            down = jnp.logical_and(zk > z, z > 0)
        go(full(k, h, 2, b, up_dev), up)
        go(full(k, h, 3, b, down_dev), down)
        go(full(k, h, 0, b, x_dev))
        go(full(k, h, 1, b, y_dev))
        if h == 1:
            go(to_core(k, b, own_ref if k == 0 else None))

    count = len(OFFSETS)

    def pick_rows():
        row = lax.broadcasted_iota(jnp.int32, (pad, 2 * half), 0)
        col = lax.broadcasted_iota(jnp.int32, (pad, 2 * half), 1)
        pick = jnp.logical_and(col == row + d * half, row < half).astype(jnp.float32).astype(jnp.bfloat16)
        width_c = pixels // 8
        for c in range(8):
            cols = pl.ds(c * width_c, width_c)
            back[0:pad, cols] = jnp.dot(pick, ref_ref[0, :, cols], preferred_element_type=jnp.float32)
        norms[...] = jnp.broadcast_to(
            jnp.sum(jnp.square(back[0:pad, :]), axis=1, keepdims=True), norms.shape
        )

    lane = lax.broadcasted_iota(jnp.int32, (8, pixels), 1) % side

    def rolled(v, dy, dx):
        amount = (dy * side) % pixels
        if dx == 0:
            return v if amount == 0 else pltpu.roll(v, amount, 1)
        plain = pltpu.roll(v, (dy * side + dx) % pixels, 1)
        wrapped = pltpu.roll(v, (dy * side + dx - dx * side) % pixels, 1)
        return jnp.where(lane == (0 if dx > 0 else side - 1), wrapped, plain)

    def build(positions):
        for pair in positions:
            group = [p for p in (2 * pair, 2 * pair + 1) if p < count]
            tiles = []
            for p in group:
                for i in range(pad // 8):
                    tiles.append((p, i))
            if len(tiles) % 2:
                tiles.append(None)
            for q in range(0, len(tiles), 2):
                parts = []
                for item in tiles[q:q + 2]:
                    if item is None:
                        parts.append(jnp.zeros((8, pixels), jnp.float32))
                    else:
                        p, i = item
                        parts.append(rolled(back[8 * i:8 * i + 8, :], *OFFSETS[p]))
                base = 2 * pair * pad + 8 * q
                shifted[base:base + 16, :] = jnp.concatenate(parts, axis=0).astype(jnp.bfloat16)

    local = pltpu.make_async_copy(own_ref, held.at[slot(cls)], own_sem)
    local.start()
    column_sends(0, 0)
    column_sends(0, 1)
    pick_rows()
    build([0])
    for k in range(PLANES):
        xb = block(order[k], y, 1 - x)
        yb = block(order[k], 1 - y, x)
        for h in range(2):
            if k + 1 < PLANES:
                arrived(h, block(order[k + 1], y, x), up_dev)
                column_sends(k + 1, h)
            arrived(h, xb, x_dev)
            if h == 1:
                go(piece(xb, part_b, x_send.at[k], b_recv, y_dev))
                go(to_core(PLANES + k, xb))
            arrived(h, yb, y_dev)
            if h == 0:
                go(piece(yb, part_a, y_send.at[k], a_recv, x_dev))
            else:
                go(to_core(2 * PLANES + k, yb))
        build([k + 1])
    for k in range(PLANES):
        b = block(order[k], 1 - y, 1 - x)
        piece(b, part_a, y_send.at[k], a_recv, x_dev).wait_recv()
        piece(b, part_b, x_send.at[k], b_recv, y_dev).wait_recv()
        go(to_core(3 * PLANES + k, b))
    local.wait()

    def core_arrival(b, carry):
        s = other * n_cls + b
        remote(held.at[s], held.at[s], part_send.at[0], part_recv.at[b], core_dev).wait_recv()
        return carry

    lax.fori_loop(0, n_cls, core_arrival, 0)
    for copy, cond in started:
        if cond is None:
            copy.wait_send()
        else:
            pl.when(cond)(lambda copy=copy: copy.wait_send())

    n_all = n_dev * rows_dev
    height = shifted.shape[0]
    meta = held[:, :, pixels:pixels + LANES].reshape(n_all, LANES)
    pick = (lax.broadcasted_iota(jnp.int32, (8, LANES), 1) == cls).astype(jnp.float32).astype(jnp.bfloat16)
    noise = lax.dot_general(pick, meta, (((1,), (1,)), ((), ())), preferred_element_type=jnp.float32)[0:1, :]
    depth = pixels // 4

    acc[...] = jnp.zeros_like(acc)

    def chunk(c, carry):
        cols = pl.ds(pl.multiple_of(c * depth, depth), depth)
        right = held[:, :, cols].reshape(n_all, depth)
        acc[...] += lax.dot_general(
            shifted[:, cols], right, (((1,), (1,)), ((), ())), preferred_element_type=jnp.float32
        )
        return carry

    lax.fori_loop(0, 4, chunk, 0)
    rows = count * pad
    prod = acc[0:rows, :].reshape(count, pad, n_all)
    offset = 0.5 * norms[:, 0:1]
    valid = jnp.logical_and(
        noise[None] > 0,
        lax.broadcasted_iota(jnp.int32, (1, pad, n_all), 1) < half,
    )
    score = jnp.where(valid, noise[None] * (prod - offset[None]), LOW)
    peak = jnp.max(jnp.max(score, axis=0), axis=0, keepdims=True)
    grown = jnp.where(valid, jnp.exp(score - peak[None]), 0.0)
    total = jnp.sum(jnp.sum(grown, axis=0), axis=0, keepdims=True)
    mine[0:1, :] = peak
    mine[1:2, :] = total
    expo[...] = grown

    def stat(j):
        t = (me + j) % n_dev
        return remote(mine, stats.at[me], st_send.at[j], st_recv.at[me], {"cls": t // 2, "dp": t % 2})

    def send_stat(j, carry):
        stat(j).start()
        return carry

    stats[me] = mine[...]
    lax.fori_loop(1, n_dev, send_stat, 0)

    def wait_stat(j, carry):
        t = (me + j) % n_dev
        remote(mine, stats.at[t], st_send.at[j], st_recv.at[t], {"cls": t // 2, "dp": t % 2}).wait_recv()
        return carry

    lax.fori_loop(1, n_dev, wait_stat, 0)

    every = stats[...]
    peaks, totals = every[:, 0:1, :], every[:, 1:2, :]
    top = jnp.max(peaks, axis=0)
    norm = jnp.sum(totals * jnp.exp(peaks - top[None]), axis=0)
    factor = jnp.exp(mine[0:1, :] - top) / norm
    weight = (expo[...] * factor[None]).reshape(rows, n_all)
    if height > rows:
        weight = jnp.concatenate([weight, jnp.zeros((height - rows, n_all), jnp.float32)], axis=0)
    weight = weight.astype(jnp.bfloat16)
    flat = jnp.sum(weight[0:rows].astype(jnp.float32).reshape(count, pad, n_all), axis=0)
    column = jnp.sum(flat, axis=1, keepdims=True)
    eye = lax.broadcasted_iota(jnp.int32, (pad, LANES), 0) == lax.broadcasted_iota(jnp.int32, (pad, LANES), 1)
    tot_ref[...] = jnp.sum(jnp.where(eye, column, 0.0), axis=0, keepdims=True)[:, 0:half]
    shifted[:, 0:n_all] = weight

    def project(c, carry):
        cols = pl.ds(pl.multiple_of(c * depth, depth), depth)
        right = held[:, :, cols].reshape(n_all, depth)
        back[:, cols] = jnp.dot(shifted[:, 0:n_all], right, preferred_element_type=jnp.float32)
        return carry

    lax.fori_loop(0, 4, project, 0)

    place = {offset: i for i, offset in enumerate(OFFSETS)}

    def tile(i):
        lines = []
        for dx in (0, 1, -1):
            line = None
            for dy in (0, 1, -1):
                base = place[(dy, dx)] * pad + 8 * i
                term = rolled(back[base:base + 8, :], -dy, 0)
                line = term if line is None else line + term
            lines.append(line)
        return lines[0] + rolled(lines[1], 0, -1) + rolled(lines[2], 0, 1)

    for i in range(pad // 8):
        keep = min(8, half - 8 * i)
        sums_ref[0, 8 * i:8 * i + keep, :] = tile(i)[0:keep]

    def end_stat(j, carry):
        stat(j).wait_send()
        return carry

    lax.fori_loop(1, n_dev, end_stat, 0)


def dense_on_device(images, references, candidates, inv_noise):
    rows_dev, pixels = images.shape
    n_cls, n_dp = lax.axis_size("cls"), lax.axis_size("dp")
    rot_count = references.shape[1]
    half = rot_count // n_dp
    pad = (half + 7) // 8 * 8
    side = math.isqrt(pixels)
    height = (len(OFFSETS) * pad + 15) // 16 * 16
    n_all = rows_dev * n_cls * n_dp
    named = (candidates[:, :, None] == jnp.arange(LANES, dtype=jnp.int32)[None, None, :]).any(axis=1)
    meta = jnp.where(named, inv_noise[:, None], jnp.zeros((), jnp.bfloat16))
    own = jnp.concatenate([images, meta], axis=1)
    width = pixels + LANES
    dma = pltpu.SemaphoreType.DMA
    vmem = pl.BlockSpec(memory_space=pltpu.VMEM)
    sums, totals = pl.pallas_call(
        functools.partial(dense_kernel, rows_dev, pixels, half, pad, side, n_cls),
        out_shape=(
            jax.ShapeDtypeStruct((1, half, pixels), jnp.float32),
            jax.ShapeDtypeStruct((1, half), jnp.float32),
        ),
        in_specs=[vmem, vmem],
        out_specs=(vmem, vmem),
        scratch_shapes=[
            pltpu.VMEM((n_cls * n_dp, rows_dev, width), jnp.bfloat16),
            pltpu.VMEM((height, pixels), jnp.bfloat16),
            pltpu.VMEM((pad, LANES), jnp.float32),
            pltpu.VMEM((height, n_all), jnp.float32),
            pltpu.VMEM((len(OFFSETS), pad, n_all), jnp.float32),
            pltpu.VMEM((height, pixels), jnp.float32),
            pltpu.VMEM((2, n_all), jnp.float32),
            pltpu.VMEM((n_cls * n_dp, 2, n_all), jnp.float32),
            dma,
            dma((PLANES, 2, 4)),
            dma((2, n_cls)),
            dma((PLANES,)),
            dma((PLANES,)),
            dma((n_cls,)),
            dma((n_cls,)),
            dma((4 * PLANES,)),
            dma((n_cls,)),
            dma((n_cls * n_dp,)),
            dma((n_cls * n_dp,)),
        ],
        compiler_params=pltpu.CompilerParams(
            collective_id=0, has_side_effects=True, vmem_limit_bytes=56 << 20
        ),
    )(own, references)
    return sums, totals


def solution(mesh):
    placed = (
        P(("cls", "dp"), None),
        P("cls", None, None),
        P(("cls", "dp"), None),
        P(("cls", "dp")),
    )
    n_cls, n_dp = mesh.shape["cls"], mesh.shape["dp"]
    dense = n_cls == PLANES * 4 and n_dp == 2
    return jax.shard_map(
        dense_on_device if dense else on_device,
        mesh=mesh,
        in_specs=placed,
        out_specs=(P("cls", "dp", None), P("cls", "dp")),
        check_vma=False,
    )
```
